32 devices in a mesh: seq: 8 (over z, y), tp: 4 (over x, core).
Axes of the slice: x: 2, y: 2, z: 4, core: 2. Of those that a mesh axis runs over, the one named last changes fastest.
Arguments:
- queries: bfloat16 [32, 2, 64, 128], P(None, None, 'tp'), may hold values from -128 to 128
- new_kv: bfloat16 [32, 2, 8, 256], P(None, None, 'tp'), may hold values from -4 to 4
- cache: bfloat16 [512, 128, 8, 256], P('seq', None, 'tp'), may hold values from -4 to 4
- table: int32 [2, 512], P(None, 'seq'), may hold values from 0 to 31, as said below
- ctx_len: int32 [32], replicated, may hold values from 2 to 2048, as said below
- out_weight: bfloat16 [8192, 8192], P('tp', 'seq'), may hold values from -0.0625 to 0.0625
Outputs:
- output: bfloat16 [32, 2, 8192], P('tp', None, 'seq')
The draws below stay inside these ranges and needn't reach their ends.
Inputs may be any that keep to these rules, and one draw needn't show every extreme that they name: `table`: each request owns exactly 64 * 8 / 32 blocks, numbered 0 upward within the request, each pair of request and number once. `ctx_len`: some request fills all of its blocks.
All inputs are finite; a program needn't handle non-finite values.
Results may differ from the reference program's by a relative error of at most 0.0051.
Values may be sent and summed in bfloat16 or wider, within the bound.
No kernel may reach another device: no remote copies, remote signals or barrier semaphores. Data moves between devices by JAX's collectives and lax.ppermute only.
A program may use at most 64 MiB of HBM per device.

```python
import jax
import jax.numpy as jnp
from jax import lax

D = 8192
QUERY_HEADS = 64
KEY_VALUE_HEADS = 8
HEAD_DIMENSION = 128
FRESH_TOKENS = 2
BLOCK_TOKENS = 128
REQUEST_COUNT = 32
BLOCKS_PER_INDEX = 64
BLOCK_COUNT = 512
N_SEQ = 8


def block_order(key):
    return jax.random.permutation(jax.random.fold_in(key, 29), BLOCK_COUNT).astype(jnp.int32)


def joint_draw(key):
    first_index, second = jax.random.split(jax.random.fold_in(key, 11), 2)
    query_group_count = QUERY_HEADS // KEY_VALUE_HEADS
    fresh_key_value = jnp.clip(jax.random.normal(first_index, (REQUEST_COUNT, FRESH_TOKENS, KEY_VALUE_HEADS, 2 * HEAD_DIMENSION), jnp.float32), -4.0, 4.0)
    base_q = jnp.clip(jax.random.normal(second, (REQUEST_COUNT, FRESH_TOKENS, QUERY_HEADS, HEAD_DIMENSION), jnp.float32), -4.0, 4.0) * 2.5
    own_keys = jnp.repeat(fresh_key_value[..., :HEAD_DIMENSION], query_group_count, axis=2)
    query = base_q + 0.7 * own_keys
    return (query, fresh_key_value)


def draw_queries(key, part):
    return joint_draw(key)[0].astype(jnp.bfloat16)


def draw_new_kv(key, part):
    return joint_draw(key)[1].astype(jnp.bfloat16)


def draw_cache(key, part):
    value_vectors = jnp.clip(jax.random.normal(jax.random.fold_in(key, 41), (BLOCK_COUNT, BLOCK_TOKENS, KEY_VALUE_HEADS, 2 * HEAD_DIMENSION), jnp.float32), -4.0, 4.0)
    return value_vectors.astype(jnp.bfloat16)


def draw_table(key, part):
    order = block_order(key)
    return jnp.stack([order % REQUEST_COUNT, order // REQUEST_COUNT]).astype(jnp.int32)


def draw_ctx_len(key, part):
    first_index, second = jax.random.split(jax.random.fold_in(key, 23))
    capacity = BLOCKS_PER_INDEX * N_SEQ // REQUEST_COUNT * BLOCK_TOKENS
    lengths = jax.random.randint(first_index, (REQUEST_COUNT,), 2, capacity + 1)
    picked = jax.random.randint(second, (), 0, REQUEST_COUNT)
    return jnp.where(jnp.arange(REQUEST_COUNT) == picked, capacity, lengths).astype(jnp.int32)


def level_of(stream_key, shape, shards, least, top_value):
    factor_of = 1.0
    for axis_at, parts in shards:
        heights = jax.random.uniform(jax.random.fold_in(jax.random.fold_in(stream_key, 6), axis_at), (parts,), jnp.float32, least / len(shards), top_value / len(shards))
        factor_of = factor_of * jnp.repeat(jnp.exp(heights), shape[axis_at] // parts).reshape((-1,) + (1,) * (len(shape) - 1 - axis_at))
    return factor_of


def scatter_about(stream_key, dims, width, bound, shards=(), kind=jnp.bfloat16):
    drawn = width * jax.random.normal(stream_key, dims, jnp.float32)
    if shards:
        drawn = drawn * level_of(stream_key, dims, shards, -0.22, 0.18)
    return jnp.clip(drawn, -bound, bound).astype(kind)


def setup_inputs(seed: int = 0) -> dict:
    splits = jax.random.split(jax.random.key(seed), 7)
    queries = draw_queries(jax.random.fold_in(splits[6], 71), 0)
    new_kv = draw_new_kv(jax.random.fold_in(splits[6], 71), 0)
    cache = draw_cache(jax.random.fold_in(splits[6], 71), 0)
    table = draw_table(jax.random.fold_in(splits[6], 71), 0)
    ctx_len = draw_ctx_len(jax.random.fold_in(splits[6], 71), 0)
    out_weight = scatter_about(splits[5], (QUERY_HEADS * HEAD_DIMENSION, D), (QUERY_HEADS * HEAD_DIMENSION) ** -0.5, 0.0625, ((0, 4), (1, 8)))
    return dict(queries=queries, new_kv=new_kv, cache=cache, table=table, ctx_len=ctx_len, out_weight=out_weight)


NEG = -1.0e30


def reference(queries, new_kv, cache, table, ctx_len, out_weight):
    query_group_count = QUERY_HEADS // KEY_VALUE_HEADS
    scaling = HEAD_DIMENSION ** -0.5
    owner_requests = table[0].astype(jnp.int32)
    number = table[1].astype(jnp.int32)
    filled = jnp.clip(ctx_len[owner_requests] - number * BLOCK_TOKENS, 0, BLOCK_TOKENS)
    is_valid = jnp.arange(BLOCK_TOKENS, dtype=jnp.int32)[None, :] < filled[:, None]
    grouped_queries = queries.astype(jnp.float32).reshape(REQUEST_COUNT, FRESH_TOKENS, KEY_VALUE_HEADS, query_group_count, HEAD_DIMENSION)

    def block_scores(owner_rows, cache_rows, valid_rows):
        picked = grouped_queries[owner_rows]
        cache_keys = cache_rows[..., :HEAD_DIMENSION].astype(jnp.float32)
        score_rows = jnp.einsum("sngrd,stgd->sngrt", picked, cache_keys, precision=lax.Precision.HIGHEST) * scaling
        return jnp.where(valid_rows[:, None, None, None, :], score_rows, NEG)

    block_contents = (owner_requests.reshape(N_SEQ, BLOCKS_PER_INDEX), cache.reshape(N_SEQ, BLOCKS_PER_INDEX, BLOCK_TOKENS, KEY_VALUE_HEADS, 2 * HEAD_DIMENSION),
                  is_valid.reshape(N_SEQ, BLOCKS_PER_INDEX, BLOCK_TOKENS))

    def block_peak(items):
        return block_scores(items[0], items[1], items[2]).max(-1)

    running_maxima = lax.map(block_peak, block_contents).reshape(BLOCK_COUNT, FRESH_TOKENS, KEY_VALUE_HEADS, query_group_count)
    fresh = jnp.einsum("angrd,amgd->angrm", grouped_queries, new_kv[..., :HEAD_DIMENSION].astype(jnp.float32),
                       precision=lax.Precision.HIGHEST) * scaling
    causal = jnp.arange(FRESH_TOKENS)[None, :] <= jnp.arange(FRESH_TOKENS)[:, None]
    fresh = jnp.where(causal[None, :, None, None, :], fresh, NEG)
    row_top = jnp.maximum(jax.ops.segment_max(running_maxima, owner_requests, num_segments=REQUEST_COUNT), fresh.max(-1))

    def block_terms(items):
        score_rows = block_scores(items[0], items[1], items[2])
        weight_rows = jnp.exp(score_rows - row_top[items[0]][..., None])
        rounded = lax.optimization_barrier(weight_rows.astype(jnp.bfloat16)).astype(jnp.float32)
        value_rows = items[1][..., HEAD_DIMENSION:].astype(jnp.float32)
        numer = jnp.einsum("sngrt,stgd->sngrd", rounded, value_rows, precision=lax.Precision.HIGHEST)
        return weight_rows.sum(-1), numer

    block_sum_parts, block_outputs = lax.map(block_terms, block_contents)
    total_sums = jax.ops.segment_sum(block_sum_parts.reshape(BLOCK_COUNT, FRESH_TOKENS, KEY_VALUE_HEADS, query_group_count), owner_requests, num_segments=REQUEST_COUNT)
    numerator_rows = jax.ops.segment_sum(block_outputs.reshape(BLOCK_COUNT, FRESH_TOKENS, KEY_VALUE_HEADS, query_group_count, HEAD_DIMENSION), owner_requests, num_segments=REQUEST_COUNT)
    fresh_weight = jnp.exp(fresh - row_top[..., None])
    total_sums = total_sums + fresh_weight.sum(-1)
    fresh_round = lax.optimization_barrier(fresh_weight.astype(jnp.bfloat16)).astype(jnp.float32)
    numerator_rows = numerator_rows + jnp.einsum("angrm,amgd->angrd", fresh_round, new_kv[..., HEAD_DIMENSION:].astype(jnp.float32),
                                 precision=lax.Precision.HIGHEST)
    attended = (numerator_rows / total_sums[..., None]).astype(jnp.bfloat16).reshape(REQUEST_COUNT * FRESH_TOKENS, QUERY_HEADS * HEAD_DIMENSION)
    result = jnp.dot(attended, out_weight, preferred_element_type=jnp.float32)
    return result.astype(jnp.bfloat16).reshape(REQUEST_COUNT, FRESH_TOKENS, D)
```

```python
import functools

import jax
import jax.numpy as jnp
from jax import lax
from jax.experimental import pallas as pl
from jax.experimental.pallas import tpu as pltpu
from jax.sharding import PartitionSpec as P

NEG = -1e30
LOG2E = 1.4426950408889634
STAT_ROWS = 16
UNROLL = 4


def iota(shape, dim):
    return lax.broadcasted_iota(jnp.int32, shape, dim)


def dot_nt(a, b):
    return lax.dot_general(a, b, (((1,), (1,)), ((), ())), preferred_element_type=jnp.float32)


def roll_pairs(x):
    parts = [pltpu.roll(x[:, c : c + 128], 2, 1) for c in range(0, x.shape[1], 128)]
    return parts[0] if len(parts) == 1 else jnp.concatenate(parts, axis=1)


def attend_kernel(
    cfg, table_in, ctx_in, q_in, fresh_in, cache, out_ref,
    table, ctx, q_ref, fresh_ref, buf, acc, top, tot, owner_of, fill_of, sem, first_sem,
):
    blocks, tokens, fresh_n, heads, kv, seq = cfg
    rows = fresh_n * heads
    group = heads // kv
    all_rows = acc.shape[0]
    chunk = all_rows // seq
    head_size = q_ref.shape[1]
    unit = head_size**-0.5 * LOG2E
    span = tokens * 2 * kv

    first = [
        pltpu.make_async_copy(src, dst, first_sem.at[i])
        for i, (src, dst) in enumerate(
            ((table_in, table), (ctx_in, ctx), (fresh_in, fresh_ref), (q_in, q_ref))
        )
    ]
    for one in first:
        one.start()
    first[0].wait()
    first[1].wait()

    def copy(block, slot):
        return pltpu.make_async_copy(cache.at[block], buf.at[slot], sem.at[slot])

    def launch(block, count):
        owner = table[0, block]
        filled = jnp.clip(ctx[owner] - table[1, block] * tokens, 0, tokens)

        @pl.when(filled > 0)
        def _():
            owner_of[count] = owner
            fill_of[count] = filled
            copy(block, count).start()

        return count + (filled > 0).astype(jnp.int32)

    used = lax.fori_loop(0, blocks, launch, jnp.int32(0))

    acc[...] = jnp.zeros_like(acc)
    tot[...] = jnp.zeros_like(tot)
    top[...] = jnp.full_like(top, NEG)

    first[2].wait()
    first[3].wait()
    home = pl.multiple_of(lax.axis_index("seq") * chunk, chunk)
    mine = pl.ds(home, chunk)
    fresh = fresh_ref[...]
    scores = dot_nt(q_ref[mine, :], fresh)
    row = iota(scores.shape, 0) + home
    col = iota(scores.shape, 1)
    per = fresh_n * 2 * kv
    keep = (
        (col // per == row // rows)
        & ((col // kv) % 2 == 0)
        & (col % kv == (row // group) % kv)
        & ((col // (2 * kv)) % fresh_n <= (row // heads) % fresh_n)
    )
    scores = jnp.where(keep, scores, NEG)
    peak = scores.max(-1, keepdims=True)
    weight = jnp.exp2((scores - peak) * unit)
    top[mine, :] = jnp.broadcast_to(peak, (chunk, 128))
    tot[mine, :] = jnp.broadcast_to(weight.sum(-1, keepdims=True), (chunk, 128))
    acc[mine, :] = jnp.dot(roll_pairs(weight).astype(jnp.bfloat16), fresh, preferred_element_type=jnp.float32)

    row = iota((rows, span), 0)
    col = iota((rows, span), 1)
    keep = ((col // kv) % 2 == 0) & (col % kv == (row // group) % kv)
    place = jnp.where(keep, col // (2 * kv), tokens)

    def step(it, carry):
        base = it * UNROLL
        for u in range(UNROLL):
            @pl.when(base + u < used)
            def _():
                copy(0, base + u).wait()

        found = []
        for u in range(UNROLL):
            slot = jnp.minimum(base + u, used - 1)
            filled = jnp.where(base + u < used, fill_of[slot], 0)
            at = pl.ds(pl.multiple_of(owner_of[slot] * rows, rows), rows)
            block = buf[slot]
            scores = jnp.where(place < filled, dot_nt(q_ref[at, :], block), NEG)
            peak = scores.max(-1, keepdims=True)
            weight = jnp.exp2((scores - peak) * unit)
            total = weight.sum(-1, keepdims=True)
            value = jnp.dot(
                roll_pairs(weight).astype(jnp.bfloat16), block, preferred_element_type=jnp.float32
            )
            found.append((at, peak, total, value))
        for at, peak, total, value in found:
            before = top[at, :]
            after = jnp.maximum(before, peak)
            old = jnp.exp2((before - after) * unit)
            new = jnp.exp2((peak - after) * unit)
            top[at, :] = after
            tot[at, :] = tot[at, :] * old + total * new
            acc[at, :] = acc[at, :] * old + value * new
        return carry

    lax.fori_loop(0, (used + UNROLL - 1) // UNROLL, step, 0)

    diagonal = iota((chunk, 128), 0) == iota((chunk, 128), 1)
    line = iota((STAT_ROWS, 128), 0)
    for d in range(seq):
        part = pl.ds(d * chunk, chunk)
        total = tot[part, :]
        some = total > 0
        safe = jnp.where(some, total, 1.0)
        out_ref[d, 0:chunk, :] = (acc[part, :] / safe).astype(jnp.bfloat16)
        level = jnp.where(some, top[part, :] * unit + jnp.log2(safe), NEG)
        flat = jnp.where(diagonal, level, 0.0).sum(0, keepdims=True)
        high = flat.astype(jnp.bfloat16).astype(jnp.float32)
        middle = (flat - high).astype(jnp.bfloat16).astype(jnp.float32)
        low = flat - high - middle
        stats = jnp.where(line == 0, high, jnp.where(line == 1, middle, jnp.where(line == 2, low, 0.0)))
        out_ref[d, chunk : chunk + STAT_ROWS, :] = stats.astype(jnp.bfloat16)


def combine_kernel(heads, in_ref, out_ref, hold):
    seq = in_ref.shape[0]
    chunk = hold.shape[0]
    stats = in_ref[:, chunk : chunk + STAT_ROWS, :].astype(jnp.float32)
    line = iota((STAT_ROWS, 128), 0)
    level = jnp.where(line < 3, stats, 0.0).sum(1)
    weight = jnp.exp2(level - level.max(0, keepdims=True))
    weight = weight / weight.sum(0, keepdims=True)
    column = jnp.transpose(weight)
    total = jnp.zeros((chunk, 128), jnp.float32)
    for s in range(seq):
        total += in_ref[s, 0:chunk, :].astype(jnp.float32) * column[0:chunk, s : s + 1]
    hold[...] = total
    count = chunk // heads
    for h in range(heads):
        picked = hold[pl.ds(h, count, stride=heads), :].astype(jnp.bfloat16)
        for s in range(seq):
            out_ref[s, :, h * 128 : (h + 1) * 128] = picked


def project_kernel(tp, x_ref, w_ref, *outs):
    mine = lax.axis_index("tp")
    y_ref = outs[-1]
    y_ref[...] = jnp.dot(x_ref[...], w_ref[...], preferred_element_type=jnp.float32)
    size = y_ref.shape[0] // tp
    for k in range(tp):
        at = pl.multiple_of((mine ^ k) * size, size)
        outs[k][...] = y_ref[pl.ds(at, size), :].astype(jnp.bfloat16)


def interleaved(x):
    *lead, kv, width = x.shape
    x = x.reshape(*lead, kv, 2, width // 2)
    return jnp.swapaxes(x, -3, -2)


def local(seq, tp, queries, new_kv, cache, table, ctx_len, out_weight):
    requests, fresh_n, heads, head_size = queries.shape
    blocks, tokens, kv, _ = cache.shape
    rows = fresh_n * heads
    all_rows = requests * rows
    chunk = all_rows // seq
    span = tokens * 2 * kv
    q = queries.reshape(all_rows, head_size)
    fresh = interleaved(new_kv).reshape(requests * fresh_n * 2 * kv, head_size)
    pages = interleaved(cache).reshape(blocks, span, head_size)
    hbm = pl.BlockSpec(memory_space=pltpu.HBM)
    vmem = pl.BlockSpec(memory_space=pltpu.VMEM)
    f32 = jnp.float32
    bf16 = jnp.bfloat16
    sent = pl.pallas_call(
        functools.partial(attend_kernel, (blocks, tokens, fresh_n, heads, kv, seq)),
        out_shape=jax.ShapeDtypeStruct((seq, chunk + STAT_ROWS, head_size), bf16),
        in_specs=[hbm] * 5,
        out_specs=vmem,
        scratch_shapes=[
            pltpu.SMEM(table.shape, jnp.int32),
            pltpu.SMEM(ctx_len.shape, jnp.int32),
            pltpu.VMEM(q.shape, bf16),
            pltpu.VMEM(fresh.shape, bf16),
            pltpu.VMEM((blocks, span, head_size), bf16),
            pltpu.VMEM((all_rows, head_size), f32),
            pltpu.VMEM((all_rows, 128), f32),
            pltpu.VMEM((all_rows, 128), f32),
            pltpu.SMEM((blocks,), jnp.int32),
            pltpu.SMEM((blocks,), jnp.int32),
            pltpu.SemaphoreType.DMA((blocks,)),
            pltpu.SemaphoreType.DMA((4,)),
        ],
        compiler_params=pltpu.CompilerParams(vmem_limit_bytes=58 << 20),
        name="attend",
    )(table, ctx_len, q, fresh, pages)
    got = lax.all_to_all(sent, "seq", 0, 0, tiled=True)
    count = chunk // heads
    copies = pl.pallas_call(
        functools.partial(combine_kernel, heads),
        out_shape=jax.ShapeDtypeStruct((seq, count, heads * head_size), bf16),
        in_specs=[vmem],
        out_specs=vmem,
        scratch_shapes=[pltpu.VMEM((chunk, head_size), f32)],
        compiler_params=pltpu.CompilerParams(vmem_limit_bytes=8 << 20),
        name="combine",
    )(got)
    attended = lax.all_to_all(copies, "seq", 0, 0, tiled=True)
    total_tokens = requests * fresh_n
    width = out_weight.shape[1]
    size = total_tokens // tp
    parts = pl.pallas_call(
        functools.partial(project_kernel, tp),
        out_shape=[jax.ShapeDtypeStruct((size, width), bf16)] * tp,
        in_specs=[vmem, vmem],
        out_specs=[vmem] * tp,
        scratch_shapes=[pltpu.VMEM((total_tokens, width), f32)],
        compiler_params=pltpu.CompilerParams(vmem_limit_bytes=16 << 20),
        name="project",
    )(attended.reshape(total_tokens, heads * head_size), out_weight)
    result = parts[0].astype(f32)
    for k in range(1, tp):
        pairs = [(j, j ^ k) for j in range(tp)]
        result = result + lax.ppermute(parts[k], "tp", pairs).astype(f32)
    return result.astype(bf16).reshape(requests // tp, fresh_n, width)


def solution(mesh):
    in_specs = (
        P(None, None, "tp", None),
        P(None, None, "tp", None),
        P("seq", None, "tp", None),
        P(None, "seq"),
        P(),
        P("tp", "seq"),
    )
    out_specs = P("tp", None, "seq")
    body = functools.partial(local, mesh.shape["seq"], mesh.shape["tp"])
    return jax.shard_map(body, mesh=mesh, in_specs=in_specs, out_specs=out_specs, check_vma=False)
```

```python
import functools

import jax
import jax.numpy as jnp
from jax import lax
from jax.experimental import pallas as pl
from jax.experimental.pallas import tpu as pltpu
from jax.sharding import PartitionSpec as P

NEG = -1e30
LOG2E = 1.4426950408889634
STAT_ROWS = 16
UNROLL = 8


def iota(shape, dim):
    return lax.broadcasted_iota(jnp.int32, shape, dim)


def dot_nt(a, b):
    return lax.dot_general(a, b, (((1,), (1,)), ((), ())), preferred_element_type=jnp.float32)


def roll_pairs(x):
    parts = [pltpu.roll(x[:, c : c + 128], 2, 1) for c in range(0, x.shape[1], 128)]
    return parts[0] if len(parts) == 1 else jnp.concatenate(parts, axis=1)


def attend_kernel(
    cfg, table_in, ctx_in, q_in, fresh_in, cache, out_ref,
    table, ctx, q_ref, fresh_ref, keys, values, acc, top, tot, owner_of, fill_of, sem, first_sem,
):
    blocks, tokens, fresh_n, heads, kv, seq = cfg
    rows = fresh_n * heads
    group = heads // kv
    all_rows = acc.shape[0]
    chunk = all_rows // seq
    head_size = q_ref.shape[1]
    unit = head_size**-0.5 * LOG2E
    span = tokens * kv

    first = [
        pltpu.make_async_copy(src, dst, first_sem.at[i])
        for i, (src, dst) in enumerate(
            ((table_in, table), (ctx_in, ctx), (fresh_in, fresh_ref), (q_in, q_ref))
        )
    ]
    for one in first:
        one.start()
    first[0].wait()
    first[1].wait()

    def copy(block, slot):
        return [
            pltpu.make_async_copy(cache.at[block, :, i], part.at[slot], sem.at[slot, i])
            for i, part in enumerate((keys, values))
        ]

    def launch(block, count):
        owner = table[0, block]
        filled = jnp.clip(ctx[owner] - table[1, block] * tokens, 0, tokens)

        @pl.when(filled > 0)
        def _():
            owner_of[count] = owner
            fill_of[count] = filled
            for one in copy(block, count):
                one.start()

        return count + (filled > 0).astype(jnp.int32)

    used = lax.fori_loop(0, blocks, launch, jnp.int32(0))

    acc[...] = jnp.zeros_like(acc)
    tot[...] = jnp.zeros_like(tot)
    top[...] = jnp.full_like(top, NEG)

    first[2].wait()
    first[3].wait()
    home = pl.multiple_of(lax.axis_index("seq") * chunk, chunk)
    mine = pl.ds(home, chunk)
    fresh = fresh_ref[...]
    scores = dot_nt(q_ref[mine, :], fresh)
    row = iota(scores.shape, 0) + home
    col = iota(scores.shape, 1)
    per = fresh_n * 2 * kv
    keep = (
        (col // per == row // rows)
        & ((col // kv) % 2 == 0)
        & (col % kv == (row // group) % kv)
        & ((col // (2 * kv)) % fresh_n <= (row // heads) % fresh_n)
    )
    scores = jnp.where(keep, scores, NEG)
    peak = scores.max(-1, keepdims=True)
    weight = jnp.exp2((scores - peak) * unit)
    top[mine, :] = jnp.broadcast_to(peak, (chunk, 128))
    tot[mine, :] = jnp.broadcast_to(weight.sum(-1, keepdims=True), (chunk, 128))
    acc[mine, :] = jnp.dot(roll_pairs(weight).astype(jnp.bfloat16), fresh, preferred_element_type=jnp.float32)

    row = iota((rows, span), 0)
    col = iota((rows, span), 1)
    keep = col % kv == (row // group) % kv
    place = jnp.where(keep, col // kv, tokens)

    def step(it, carry):
        base = it * UNROLL
        for u in range(UNROLL):
            @pl.when(base + u < used)
            def _():
                for one in copy(0, base + u):
                    one.wait()

        slots, places, scores, weights, found = [], [], [], [], []
        for u in range(UNROLL):
            slot = jnp.minimum(base + u, used - 1)
            at = pl.ds(pl.multiple_of(owner_of[slot] * rows, rows), rows)
            slots.append(slot)
            places.append(at)
            scores.append(dot_nt(q_ref[at, :], keys[slot].reshape(span, head_size)))
        for u in range(UNROLL):
            filled = jnp.where(base + u < used, fill_of[slots[u]], 0)
            score = jnp.where(place < filled, scores[u], NEG)
            peak = score.max(-1, keepdims=True)
            weight = jnp.exp2((score - peak) * unit)
            weights.append(weight.astype(jnp.bfloat16))
            found.append((places[u], peak, weight.sum(-1, keepdims=True)))
        outs = [
            jnp.dot(weights[u], values[slots[u]].reshape(span, head_size), preferred_element_type=jnp.float32)
            for u in range(UNROLL)
        ]
        for (at, peak, total), value in zip(found, outs):
            before = top[at, :]
            after = jnp.maximum(before, peak)
            old = jnp.exp2((before - after) * unit)
            new = jnp.exp2((peak - after) * unit)
            top[at, :] = after
            tot[at, :] = tot[at, :] * old + total * new
            acc[at, :] = acc[at, :] * old + value * new
        return carry

    lax.fori_loop(0, (used + UNROLL - 1) // UNROLL, step, 0)

    diagonal = iota((chunk, 128), 0) == iota((chunk, 128), 1)
    line = iota((STAT_ROWS, 128), 0)
    for d in range(seq):
        part = pl.ds(d * chunk, chunk)
        total = tot[part, :]
        some = total > 0
        safe = jnp.where(some, total, 1.0)
        out_ref[d, 0:chunk, :] = (acc[part, :] / safe).astype(jnp.bfloat16)
        level = jnp.where(some, top[part, :] * unit + jnp.log2(safe), NEG)
        flat = jnp.where(diagonal, level, 0.0).sum(0, keepdims=True)
        high = flat.astype(jnp.bfloat16).astype(jnp.float32)
        middle = (flat - high).astype(jnp.bfloat16).astype(jnp.float32)
        low = flat - high - middle
        stats = jnp.where(line == 0, high, jnp.where(line == 1, middle, jnp.where(line == 2, low, 0.0)))
        out_ref[d, chunk : chunk + STAT_ROWS, :] = stats.astype(jnp.bfloat16)


def combine_kernel(heads, in_ref, out_ref, hold):
    seq = in_ref.shape[0]
    chunk = hold.shape[0]
    stats = in_ref[:, chunk : chunk + STAT_ROWS, :].astype(jnp.float32)
    line = iota((STAT_ROWS, 128), 0)
    level = jnp.where(line < 3, stats, 0.0).sum(1)
    weight = jnp.exp2(level - level.max(0, keepdims=True))
    weight = weight / weight.sum(0, keepdims=True)
    column = jnp.transpose(weight)
    total = jnp.zeros((chunk, 128), jnp.float32)
    for s in range(seq):
        total += in_ref[s, 0:chunk, :].astype(jnp.float32) * column[0:chunk, s : s + 1]
    hold[...] = total
    count = chunk // heads
    for h in range(heads):
        picked = hold[pl.ds(h, count, stride=heads), :].astype(jnp.bfloat16)
        for s in range(seq):
            out_ref[s, :, h * 128 : (h + 1) * 128] = picked


def project_kernel(tp, x_ref, w_ref, *outs):
    mine = lax.axis_index("tp")
    y_ref = outs[-1]
    y_ref[...] = jnp.dot(x_ref[...], w_ref[...], preferred_element_type=jnp.float32)
    size = y_ref.shape[0] // tp
    for k in range(tp):
        at = pl.multiple_of((mine ^ k) * size, size)
        outs[k][...] = y_ref[pl.ds(at, size), :].astype(jnp.bfloat16)


def interleaved(x):
    *lead, kv, width = x.shape
    x = x.reshape(*lead, kv, 2, width // 2)
    return jnp.swapaxes(x, -3, -2)


def local(seq, tp, queries, new_kv, cache, table, ctx_len, out_weight):
    requests, fresh_n, heads, head_size = queries.shape
    blocks, tokens, kv, _ = cache.shape
    rows = fresh_n * heads
    all_rows = requests * rows
    chunk = all_rows // seq
    q = queries.reshape(all_rows, head_size)
    fresh = interleaved(new_kv).reshape(requests * fresh_n * 2 * kv, head_size)
    pages = interleaved(cache)
    hbm = pl.BlockSpec(memory_space=pltpu.HBM)
    vmem = pl.BlockSpec(memory_space=pltpu.VMEM)
    f32 = jnp.float32
    bf16 = jnp.bfloat16
    sent = pl.pallas_call(
        functools.partial(attend_kernel, (blocks, tokens, fresh_n, heads, kv, seq)),
        out_shape=jax.ShapeDtypeStruct((seq, chunk + STAT_ROWS, head_size), bf16),
        in_specs=[hbm] * 5,
        out_specs=vmem,
        scratch_shapes=[
            pltpu.SMEM(table.shape, jnp.int32),
            pltpu.SMEM(ctx_len.shape, jnp.int32),
            pltpu.VMEM(q.shape, bf16),
            pltpu.VMEM(fresh.shape, bf16),
            pltpu.VMEM((blocks, tokens, kv, head_size), bf16),
            pltpu.VMEM((blocks, tokens, kv, head_size), bf16),
            pltpu.VMEM((all_rows, head_size), f32),
            pltpu.VMEM((all_rows, 128), f32),
            pltpu.VMEM((all_rows, 128), f32),
            pltpu.SMEM((blocks,), jnp.int32),
            pltpu.SMEM((blocks,), jnp.int32),
            pltpu.SemaphoreType.DMA((blocks, 2)),
            pltpu.SemaphoreType.DMA((4,)),
        ],
        compiler_params=pltpu.CompilerParams(vmem_limit_bytes=58 << 20),
        name="attend",
    )(table, ctx_len, q, fresh, pages)
    got = lax.all_to_all(sent, "seq", 0, 0, tiled=True)
    count = chunk // heads
    copies = pl.pallas_call(
        functools.partial(combine_kernel, heads),
        out_shape=jax.ShapeDtypeStruct((seq, count, heads * head_size), bf16),
        in_specs=[vmem],
        out_specs=vmem,
        scratch_shapes=[pltpu.VMEM((chunk, head_size), f32)],
        compiler_params=pltpu.CompilerParams(vmem_limit_bytes=8 << 20),
        name="combine",
    )(got)
    attended = lax.all_to_all(copies, "seq", 0, 0, tiled=True)
    total_tokens = requests * fresh_n
    width = out_weight.shape[1]
    size = total_tokens // tp
    parts = pl.pallas_call(
        functools.partial(project_kernel, tp),
        out_shape=[jax.ShapeDtypeStruct((size, width), bf16)] * tp,
        in_specs=[vmem, vmem],
        out_specs=[vmem] * tp,
        scratch_shapes=[pltpu.VMEM((total_tokens, width), f32)],
        compiler_params=pltpu.CompilerParams(vmem_limit_bytes=16 << 20),
        name="project",
    )(attended.reshape(total_tokens, heads * head_size), out_weight)
    result = parts[0].astype(f32)
    for k in range(1, tp):
        pairs = [(j, j ^ k) for j in range(tp)]
        result = result + lax.ppermute(parts[k], "tp", pairs).astype(f32)
    return result.astype(bf16).reshape(requests // tp, fresh_n, width)


def solution(mesh):
    in_specs = (
        P(None, None, "tp", None),
        P(None, None, "tp", None),
        P("seq", None, "tp", None),
        P(None, "seq"),
        P(),
        P("tp", "seq"),
    )
    out_specs = P("tp", None, "seq")
    body = functools.partial(local, mesh.shape["seq"], mesh.shape["tp"])
    return jax.shard_map(body, mesh=mesh, in_specs=in_specs, out_specs=out_specs, check_vma=False)
```

```python
import functools

import jax
import jax.numpy as jnp
from jax import lax
from jax.experimental import pallas as pl
from jax.experimental.pallas import tpu as pltpu
from jax.sharding import PartitionSpec as P

NEG = -1e30
LOG2E = 1.4426950408889634
STAT_ROWS = 8
UNROLL = 8


def iota(shape, dim):
    return lax.broadcasted_iota(jnp.int32, shape, dim)


def dot_nt(a, b):
    return lax.dot_general(a, b, (((1,), (1,)), ((), ())), preferred_element_type=jnp.float32)


def over(x, n):
    return x >> (n.bit_length() - 1) if n & (n - 1) == 0 else x // n


def left(x, n):
    return x & (n - 1) if n & (n - 1) == 0 else x % n


def roll_pairs(x):
    parts = [pltpu.roll(x[:, c : c + 128], 2, 1) for c in range(0, x.shape[1], 128)]
    return parts[0] if len(parts) == 1 else jnp.concatenate(parts, axis=1)


def attend_kernel(
    cfg, table_in, ctx_in, q_in, fresh_in, cache, out_ref,
    table, ctx, q_ref, fresh_ref, keys, values, acc, top, tot, owner_of, fill_of, sem, first_sem,
):
    blocks, tokens, fresh_n, heads, kv, seq = cfg
    rows = fresh_n * heads
    group = heads // kv
    all_rows = acc.shape[0]
    chunk = all_rows // seq
    head_size = q_ref.shape[1]
    unit = head_size**-0.5 * LOG2E
    span = tokens * kv

    first = [
        pltpu.make_async_copy(src, dst, first_sem.at[i])
        for i, (src, dst) in enumerate(
            ((table_in, table), (ctx_in, ctx), (fresh_in, fresh_ref), (q_in, q_ref))
        )
    ]
    for one in first:
        one.start()
    first[0].wait()
    first[1].wait()

    def copy(block, slot):
        return [
            pltpu.make_async_copy(cache.reshape(blocks, span, 2 * head_size).at[block, :, pl.ds(i * head_size, head_size)], part.at[slot], sem.at[slot, i])
            for i, part in enumerate((keys, values))
        ]

    def launch(block, count):
        owner = table[0, block]
        filled = jnp.clip(ctx[owner] - table[1, block] * tokens, 0, tokens)

        @pl.when(filled > 0)
        def _():
            owner_of[count] = owner
            fill_of[count] = filled
            for one in copy(block, count):
                one.start()

        return count + (filled > 0).astype(jnp.int32)

    used = lax.fori_loop(0, blocks, launch, jnp.int32(0), unroll=8)

    acc[...] = jnp.zeros_like(acc)
    tot[...] = jnp.zeros_like(tot)
    top[...] = jnp.full_like(top, NEG)

    first[2].wait()
    first[3].wait()
    home = pl.multiple_of(lax.axis_index("seq") * chunk, chunk)
    mine = pl.ds(home, chunk)
    per = fresh_n * 2 * kv
    window = min(fresh_ref.shape[0], max(128, chunk // rows * per))
    skip = pl.multiple_of(over(over(home, rows) * per, window) * window, window)
    fresh = fresh_ref[pl.ds(skip, window), :]
    scores = dot_nt(q_ref[mine, :], fresh)
    row = iota(scores.shape, 0) + home
    col = iota(scores.shape, 1) + skip
    keep = (
        (over(col, per) == over(row, rows))
        & (left(over(col, kv), 2) == 0)
        & (left(col, kv) == left(over(row, group), kv))
        & (left(over(col, 2 * kv), fresh_n) <= left(over(row, heads), fresh_n))
    )
    scores = jnp.where(keep, scores, NEG)
    peak = scores.max(-1, keepdims=True)
    weight = jnp.exp2((scores - peak) * unit)
    top[mine, :] = jnp.broadcast_to(peak, (chunk, 128))
    tot[mine, :] = jnp.broadcast_to(weight.sum(-1, keepdims=True), (chunk, 128))
    acc[mine, :] = jnp.dot(roll_pairs(weight).astype(jnp.bfloat16), fresh, preferred_element_type=jnp.float32)

    row = iota((rows, span), 0)
    col = iota((rows, span), 1)
    keep = left(col, kv) == left(over(row, group), kv)
    place = jnp.where(keep, over(col, kv), tokens)

    def step(it, carry):
        base = it * UNROLL
        for u in range(UNROLL):
            @pl.when(base + u < used)
            def _():
                for one in copy(0, base + u):
                    one.wait()

        slots, places, scores, weights, found = [], [], [], [], []
        for u in range(UNROLL):
            slot = jnp.minimum(base + u, used - 1)
            at = pl.ds(pl.multiple_of(owner_of[slot] * rows, rows), rows)
            slots.append(slot)
            places.append(at)
            scores.append(dot_nt(q_ref[at, :], keys[slot]))
        for u in range(UNROLL):
            filled = jnp.where(base + u < used, fill_of[slots[u]], 0)
            score = jnp.where(place < filled, scores[u], NEG)
            peak = score.max(-1, keepdims=True)
            weight = jnp.exp2((score - peak) * unit)
            weights.append(weight.astype(jnp.bfloat16))
            found.append((places[u], peak, weight.sum(-1, keepdims=True)))
        outs = [
            jnp.dot(weights[u], values[slots[u]], preferred_element_type=jnp.float32)
            for u in range(UNROLL)
        ]
        for (at, peak, total), value in zip(found, outs):
            before = top[at, :]
            after = jnp.maximum(before, peak)
            old = jnp.exp2((before - after) * unit)
            new = jnp.exp2((peak - after) * unit)
            top[at, :] = after
            tot[at, :] = tot[at, :] * old + total * new
            acc[at, :] = acc[at, :] * old + value * new
        return carry

    lax.fori_loop(0, (used + UNROLL - 1) // UNROLL, step, 0)

    diagonal = iota((chunk, 128), 0) == iota((chunk, 128), 1)
    line = iota((STAT_ROWS, 128), 0)
    for d in range(seq):
        part = pl.ds(d * chunk, chunk)
        out_ref[d, 0:chunk, :] = acc[part, :].astype(jnp.bfloat16)
        stats = jnp.zeros((STAT_ROWS, 128), jnp.float32)
        for i, ref in enumerate((top, tot)):
            rest = jnp.where(diagonal, ref[part, :], 0.0).sum(0, keepdims=True)
            for j in range(3):
                piece = rest.astype(jnp.bfloat16).astype(jnp.float32)
                stats = jnp.where(line == 3 * i + j, piece, stats)
                rest = rest - piece
        out_ref[d, chunk : chunk + STAT_ROWS, :] = stats.astype(jnp.bfloat16)


def combine_kernel(heads, unit, in_ref, out_ref, hold):
    seq = in_ref.shape[0]
    chunk = hold.shape[0]
    stats = in_ref[:, chunk : chunk + STAT_ROWS, :].astype(jnp.float32)
    line = iota((STAT_ROWS, 128), 0)
    peak = jnp.where(line < 3, stats, 0.0).sum(1)
    total = jnp.where((line >= 3) & (line < 6), stats, 0.0).sum(1)
    weight = jnp.exp2((peak - peak.max(0, keepdims=True)) * unit)
    weight = weight / (weight * total).sum(0, keepdims=True)
    column = jnp.transpose(weight)
    total = jnp.zeros((chunk, 128), jnp.float32)
    for s in range(seq):
        total += in_ref[s, 0:chunk, :].astype(jnp.float32) * column[0:chunk, s : s + 1]
    hold[...] = total
    count = chunk // heads
    for h in range(heads):
        picked = hold[pl.ds(h, count, stride=heads), :].astype(jnp.bfloat16)
        for s in range(seq):
            out_ref[s, :, h * 128 : (h + 1) * 128] = picked


def project_kernel(tp, x_ref, w_ref, *outs):
    mine = lax.axis_index("tp")
    y_ref = outs[-1]
    y_ref[...] = jnp.dot(x_ref[...], w_ref[...], preferred_element_type=jnp.float32)
    size = y_ref.shape[0] // tp
    for k in range(tp):
        at = pl.multiple_of((mine ^ k) * size, size)
        outs[k][...] = y_ref[pl.ds(at, size), :].astype(jnp.bfloat16)


def interleaved(x):
    *lead, kv, width = x.shape
    x = x.reshape(*lead, kv, 2, width // 2)
    return jnp.swapaxes(x, -3, -2)


def local(seq, tp, queries, new_kv, cache, table, ctx_len, out_weight):
    requests, fresh_n, heads, head_size = queries.shape
    blocks, tokens, kv, _ = cache.shape
    rows = fresh_n * heads
    all_rows = requests * rows
    chunk = all_rows // seq
    q = queries.reshape(all_rows, head_size)
    fresh = interleaved(new_kv).reshape(requests * fresh_n * 2 * kv, head_size)
    pages = cache
    hbm = pl.BlockSpec(memory_space=pltpu.HBM)
    vmem = pl.BlockSpec(memory_space=pltpu.VMEM)
    f32 = jnp.float32
    bf16 = jnp.bfloat16
    sent = pl.pallas_call(
        functools.partial(attend_kernel, (blocks, tokens, fresh_n, heads, kv, seq)),
        out_shape=jax.ShapeDtypeStruct((seq, chunk + STAT_ROWS, head_size), bf16),
        in_specs=[hbm] * 5,
        out_specs=vmem,
        scratch_shapes=[
            pltpu.SMEM(table.shape, jnp.int32),
            pltpu.SMEM(ctx_len.shape, jnp.int32),
            pltpu.VMEM(q.shape, bf16),
            pltpu.VMEM(fresh.shape, bf16),
            pltpu.VMEM((blocks, tokens * kv, head_size), bf16),
            pltpu.VMEM((blocks, tokens * kv, head_size), bf16),
            pltpu.VMEM((all_rows, head_size), f32),
            pltpu.VMEM((all_rows, 128), f32),
            pltpu.VMEM((all_rows, 128), f32),
            pltpu.SMEM((blocks,), jnp.int32),
            pltpu.SMEM((blocks,), jnp.int32),
            pltpu.SemaphoreType.DMA((blocks, 2)),
            pltpu.SemaphoreType.DMA((4,)),
        ],
        compiler_params=pltpu.CompilerParams(vmem_limit_bytes=24 << 20),
        name="attend",
    )(*[pltpu.with_memory_space_constraint(x, pltpu.HBM) for x in (table, ctx_len, q, fresh, pages)])
    got = lax.all_to_all(sent, "seq", 0, 0, tiled=True)
    count = chunk // heads
    copies = pl.pallas_call(
        functools.partial(combine_kernel, heads, head_size**-0.5 * LOG2E),
        out_shape=jax.ShapeDtypeStruct((seq, count, heads * head_size), bf16),
        in_specs=[vmem],
        out_specs=vmem,
        scratch_shapes=[pltpu.VMEM((chunk, head_size), f32)],
        compiler_params=pltpu.CompilerParams(vmem_limit_bytes=8 << 20),
        name="combine",
    )(got)
    attended = lax.all_to_all(copies, "seq", 0, 0, tiled=True)
    total_tokens = requests * fresh_n
    width = out_weight.shape[1]
    size = total_tokens // tp
    parts = pl.pallas_call(
        functools.partial(project_kernel, tp),
        out_shape=[jax.ShapeDtypeStruct((size, width), bf16)] * tp,
        in_specs=[vmem, vmem],
        out_specs=[vmem] * tp,
        scratch_shapes=[pltpu.VMEM((total_tokens, width), f32)],
        compiler_params=pltpu.CompilerParams(vmem_limit_bytes=16 << 20),
        name="project",
    )(attended.reshape(total_tokens, heads * head_size), out_weight)
    result = parts[0].astype(f32)
    for k in range(tp - 1, 0, -1):
        pairs = [(j, j ^ k) for j in range(tp)]
        result = result + lax.ppermute(parts[k], "tp", pairs).astype(f32)
    return result.astype(bf16).reshape(requests // tp, fresh_n, width)


def solution(mesh):
    in_specs = (
        P(None, None, "tp", None),
        P(None, None, "tp", None),
        P("seq", None, "tp", None),
        P(None, "seq"),
        P(),
        P("tp", "seq"),
    )
    out_specs = P("tp", None, "seq")
    body = functools.partial(local, mesh.shape["seq"], mesh.shape["tp"])
    return jax.shard_map(body, mesh=mesh, in_specs=in_specs, out_specs=out_specs, check_vma=False)
```

```python
import functools

import jax
import jax.numpy as jnp
from jax import lax
from jax.experimental import pallas as pl
from jax.experimental.pallas import tpu as pltpu
from jax.sharding import PartitionSpec as P

NEG = -1e30
LOG2E = 1.4426950408889634
STAT_ROWS = 8
UNROLL = 8
LAUNCH_UNROLL = 8


def iota(shape, dim):
    return lax.broadcasted_iota(jnp.int32, shape, dim)


def dot_nt(a, b):
    return lax.dot_general(a, b, (((1,), (1,)), ((), ())), preferred_element_type=jnp.float32)


def over(x, n):
    return x >> (n.bit_length() - 1) if n & (n - 1) == 0 else x // n


def left(x, n):
    return x & (n - 1) if n & (n - 1) == 0 else x % n


def roll_pairs(x):
    parts = [pltpu.roll(x[:, c : c + 128], 2, 1) for c in range(0, x.shape[1], 128)]
    return parts[0] if len(parts) == 1 else jnp.concatenate(parts, axis=1)


def attend_kernel(
    cfg, table_in, ctx_in, q_in, fresh_in, cache, out_ref,
    table, ctx, q_ref, fresh_ref, buf, acc, top, tot, owner_of, fill_of, sem, first_sem,
):
    blocks, tokens, fresh_n, heads, kv, seq = cfg
    rows = fresh_n * heads
    group = heads // kv
    all_rows = acc.shape[0]
    chunk = all_rows // seq
    head_size = q_ref.shape[1]
    unit = head_size**-0.5 * LOG2E
    span = tokens * kv

    first = [
        pltpu.make_async_copy(src, dst, first_sem.at[i])
        for i, (src, dst) in enumerate(
            ((table_in, table), (ctx_in, ctx), (fresh_in, fresh_ref), (q_in, q_ref))
        )
    ]
    for one in first:
        one.start()
    acc[...] = jnp.zeros_like(acc)
    tot[...] = jnp.zeros_like(tot)
    top[...] = jnp.full_like(top, NEG)
    first[0].wait()
    first[1].wait()
    pages = cache.reshape(blocks, span, 2 * head_size)

    def launch(block, count):
        owner = table[0, block]
        filled = jnp.clip(ctx[owner] - table[1, block] * tokens, 0, tokens)

        @pl.when(filled > 0)
        def _():
            owner_of[count] = owner
            fill_of[count] = filled
            ready = sem.at[over(count, UNROLL)]
            for i in range(2):
                part = pages.at[block, :, pl.ds(i * head_size, head_size)]
                pltpu.make_async_copy(part, buf.at[count, i], ready).start()

        return count + (filled > 0).astype(jnp.int32)

    used = lax.fori_loop(0, blocks, launch, jnp.int32(0), unroll=LAUNCH_UNROLL)

    first[2].wait()
    first[3].wait()
    home = pl.multiple_of(lax.axis_index("seq") * chunk, chunk)
    mine = pl.ds(home, chunk)
    per = fresh_n * 2 * kv
    window = min(fresh_ref.shape[0], max(128, chunk // rows * per))
    skip = pl.multiple_of(over(over(home, rows) * per, window) * window, window)
    fresh = fresh_ref[pl.ds(skip, window), :]
    scores = dot_nt(q_ref[mine, :], fresh)
    row = iota(scores.shape, 0) + home
    col = iota(scores.shape, 1) + skip
    keep = (
        (over(col, per) == over(row, rows))
        & (left(over(col, kv), 2) == 0)
        & (left(col, kv) == left(over(row, group), kv))
        & (left(over(col, 2 * kv), fresh_n) <= left(over(row, heads), fresh_n))
    )
    scores = jnp.where(keep, scores, NEG)
    peak = scores.max(-1, keepdims=True)
    weight = jnp.exp2((scores - peak) * unit)
    top[mine, :] = jnp.broadcast_to(peak, (chunk, 128))
    tot[mine, :] = jnp.broadcast_to(weight.sum(-1, keepdims=True), (chunk, 128))
    acc[mine, :] = jnp.dot(roll_pairs(weight).astype(jnp.bfloat16), fresh, preferred_element_type=jnp.float32)

    row = iota((rows, span), 0)
    col = iota((rows, span), 1)
    keep = left(col, kv) == left(over(row, group), kv)
    place = jnp.where(keep, over(col, kv), tokens)

    def step(it, carry):
        base = it * UNROLL

        def arrived(view):
            pltpu.make_async_copy(view, view, sem.at[it]).wait()

        whole = base + UNROLL <= used

        @pl.when(whole)
        def _():
            arrived(buf.at[pl.ds(base, UNROLL)])

        @pl.when(jnp.logical_not(whole))
        def _():
            lax.fori_loop(base, used, lambda slot, c: (arrived(buf.at[slot]), c)[1], 0)

        slots, places, scores, weights, found = [], [], [], [], []
        for u in range(UNROLL):
            slot = jnp.minimum(base + u, used - 1)
            at = pl.ds(pl.multiple_of(owner_of[slot] * rows, rows), rows)
            slots.append(slot)
            places.append(at)
            scores.append(dot_nt(q_ref[at, :], buf[slot, 0]))
        for u in range(UNROLL):
            filled = jnp.where(base + u < used, fill_of[slots[u]], 0)
            score = jnp.where(place < filled, scores[u], NEG)
            peak = score.max(-1, keepdims=True)
            weight = jnp.exp2((score - peak) * unit)
            weights.append(weight.astype(jnp.bfloat16))
            found.append((places[u], peak, weight.sum(-1, keepdims=True)))
        outs = [
            jnp.dot(weights[u], buf[slots[u], 1], preferred_element_type=jnp.float32)
            for u in range(UNROLL)
        ]
        scales = []
        for at, peak, _ in found:
            before = top[at, :]
            after = jnp.maximum(before, peak)
            top[at, :] = after
            scales.append((before - after, peak - after))
        scales = [(jnp.exp2(old * unit), jnp.exp2(new * unit)) for old, new in scales]
        for (at, _, total), value, (old, new) in zip(found, outs, scales):
            tot[at, :] = tot[at, :] * old + total * new
            acc[at, :] = acc[at, :] * old + value * new
        return carry

    lax.fori_loop(0, (used + UNROLL - 1) // UNROLL, step, 0)

    diagonal = iota((chunk, 128), 0) == iota((chunk, 128), 1)
    line = iota((STAT_ROWS, 128), 0)
    for d in range(seq):
        part = pl.ds(d * chunk, chunk)
        out_ref[d, 0:chunk, :] = acc[part, :].astype(jnp.bfloat16)
        stats = jnp.zeros((STAT_ROWS, 128), jnp.float32)
        for i, ref in enumerate((top, tot)):
            rest = jnp.where(diagonal, ref[part, :], 0.0).sum(0, keepdims=True)
            for j in range(3):
                piece = rest.astype(jnp.bfloat16).astype(jnp.float32)
                stats = jnp.where(line == 3 * i + j, piece, stats)
                rest = rest - piece
        out_ref[d, chunk : chunk + STAT_ROWS, :] = stats.astype(jnp.bfloat16)


def combine_kernel(heads, unit, in_ref, out_ref, hold):
    seq = in_ref.shape[0]
    chunk = hold.shape[0]
    stats = in_ref[:, chunk : chunk + STAT_ROWS, :].astype(jnp.float32)
    line = iota((STAT_ROWS, 128), 0)
    peak = jnp.where(line < 3, stats, 0.0).sum(1)
    total = jnp.where((line >= 3) & (line < 6), stats, 0.0).sum(1)
    weight = jnp.exp2((peak - peak.max(0, keepdims=True)) * unit)
    weight = weight / (weight * total).sum(0, keepdims=True)
    column = jnp.transpose(weight)
    total = jnp.zeros((chunk, 128), jnp.float32)
    for s in range(seq):
        total += in_ref[s, 0:chunk, :].astype(jnp.float32) * column[0:chunk, s : s + 1]
    hold[...] = total
    count = chunk // heads
    for h in range(heads):
        picked = hold[pl.ds(h, count, stride=heads), :].astype(jnp.bfloat16)
        for s in range(seq):
            out_ref[s, :, h * 128 : (h + 1) * 128] = picked


def project_kernel(tp, x_ref, w_ref, *outs):
    mine = lax.axis_index("tp")
    y_ref = outs[-1]
    y_ref[...] = jnp.dot(x_ref[...], w_ref[...], preferred_element_type=jnp.float32)
    size = y_ref.shape[0] // tp
    for k in range(tp):
        at = pl.multiple_of((mine ^ k) * size, size)
        outs[k][...] = y_ref[pl.ds(at, size), :].astype(jnp.bfloat16)


def interleaved(x):
    *lead, kv, width = x.shape
    x = x.reshape(*lead, kv, 2, width // 2)
    return jnp.swapaxes(x, -3, -2)


def local(seq, tp, queries, new_kv, cache, table, ctx_len, out_weight):
    requests, fresh_n, heads, head_size = queries.shape
    blocks, tokens, kv, _ = cache.shape
    rows = fresh_n * heads
    all_rows = requests * rows
    chunk = all_rows // seq
    q = queries.reshape(all_rows, head_size)
    fresh = interleaved(new_kv).reshape(requests * fresh_n * 2 * kv, head_size)
    pages = cache
    hbm = pl.BlockSpec(memory_space=pltpu.HBM)
    vmem = pl.BlockSpec(memory_space=pltpu.VMEM)
    f32 = jnp.float32
    bf16 = jnp.bfloat16
    sent = pl.pallas_call(
        functools.partial(attend_kernel, (blocks, tokens, fresh_n, heads, kv, seq)),
        out_shape=jax.ShapeDtypeStruct((seq, chunk + STAT_ROWS, head_size), bf16),
        in_specs=[hbm] * 5,
        out_specs=vmem,
        scratch_shapes=[
            pltpu.SMEM(table.shape, jnp.int32),
            pltpu.SMEM(ctx_len.shape, jnp.int32),
            pltpu.VMEM(q.shape, bf16),
            pltpu.VMEM(fresh.shape, bf16),
            pltpu.VMEM((blocks, 2, tokens * kv, head_size), bf16),
            pltpu.VMEM((all_rows, head_size), f32),
            pltpu.VMEM((all_rows, 128), f32),
            pltpu.VMEM((all_rows, 128), f32),
            pltpu.SMEM((blocks,), jnp.int32),
            pltpu.SMEM((blocks,), jnp.int32),
            pltpu.SemaphoreType.DMA((pl.cdiv(blocks, UNROLL),)),
            pltpu.SemaphoreType.DMA((4,)),
        ],
        compiler_params=pltpu.CompilerParams(vmem_limit_bytes=24 << 20),
        name="attend",
    )(*[pltpu.with_memory_space_constraint(x, pltpu.HBM) for x in (table, ctx_len, q, fresh, pages)])
    got = lax.all_to_all(sent, "seq", 0, 0, tiled=True)
    count = chunk // heads
    copies = pl.pallas_call(
        functools.partial(combine_kernel, heads, head_size**-0.5 * LOG2E),
        out_shape=jax.ShapeDtypeStruct((seq, count, heads * head_size), bf16),
        in_specs=[vmem],
        out_specs=vmem,
        scratch_shapes=[pltpu.VMEM((chunk, head_size), f32)],
        compiler_params=pltpu.CompilerParams(vmem_limit_bytes=8 << 20),
        name="combine",
    )(got)
    attended = lax.all_to_all(copies, "seq", 0, 0, tiled=True)
    total_tokens = requests * fresh_n
    width = out_weight.shape[1]
    size = total_tokens // tp
    parts = pl.pallas_call(
        functools.partial(project_kernel, tp),
        out_shape=[jax.ShapeDtypeStruct((size, width), bf16)] * tp,
        in_specs=[vmem, vmem],
        out_specs=[vmem] * tp,
        scratch_shapes=[pltpu.VMEM((total_tokens, width), f32)],
        compiler_params=pltpu.CompilerParams(vmem_limit_bytes=16 << 20),
        name="project",
    )(attended.reshape(total_tokens, heads * head_size), out_weight)
    result = parts[0].astype(f32)
    for k in range(tp - 1, 0, -1):
        pairs = [(j, j ^ k) for j in range(tp)]
        result = result + lax.ppermute(parts[k], "tp", pairs).astype(f32)
    return result.astype(bf16).reshape(requests // tp, fresh_n, width)


def solution(mesh):
    in_specs = (
        P(None, None, "tp", None),
        P(None, None, "tp", None),
        P("seq", None, "tp", None),
        P(None, "seq"),
        P(),
        P("tp", "seq"),
    )
    out_specs = P("tp", None, "seq")
    body = functools.partial(local, mesh.shape["seq"], mesh.shape["tp"])
    return jax.shard_map(body, mesh=mesh, in_specs=in_specs, out_specs=out_specs, check_vma=False)
```
